32 devices in a mesh: apa: 2 (over y), gz: 4 (over x, core), drift: 4 (over z).
Axes of the slice: x: 2, y: 2, z: 4, core: 2. Of those that a mesh axis runs over, the one named last changes fastest.
Arguments:
- charge: bfloat16 [16384, 384], P(('apa', 'gz', 'drift')), parts along dimension 0, may hold values from 0.049804688 to 2
- intersection: bfloat16 [128, 3, 2, 32, 128], P(('apa', 'gz', 'drift')), parts along dimension 0, may hold values from 0 to 0.03125
- ovl_block: int32 [128, 3, 2], P(('apa', 'gz', 'drift')), parts along dimension 0, may hold values from 0 to 15, as said below
- ovl_count: int32 [128, 3], P(('apa', 'gz', 'drift')), parts along dimension 0, may hold values from 1 to 2
- diff_class: int32 [768], P('apa'), parts along dimension 0, may hold values from 0 to 5
- response: bfloat16 [3, 21, 200], replicated, may hold values from -0.029907227 to 0.029907227
- cotangent: bfloat16 [6, 512, 3072], P('apa', 'gz', 'drift'), parts along dimension 0, may hold values from -120 to 120
Outputs:
- signal: bfloat16 [6, 512, 3072], P('apa', 'gz', 'drift'), parts along dimension 0
- charge_grad: bfloat16 [16384, 384], P(('apa', 'gz', 'drift')), parts along dimension 0
The draws below stay inside these ranges and needn't reach their ends.
There are 2 independent parts, one for each index of `apa`. The reference program is written for one: setup_inputs(seed, part) draws one part's arguments, and reference() takes and returns one part's arrays. A program takes and returns all parts, laid end to end along the dimension named above; an argument that names none is the same for every part. Nothing has to cross between parts.
Inputs may be any that keep to these rules, and one draw needn't show every extreme that they name: `ovl_block`: planes are U, V, W in this order. Cell block b lies in z-block b // 16; its W entries name wire blocks of that z-block, z-block g owning wire blocks g * 4 to (g + 1) * 4 - 1 of every plane. Entry 0 of each list is live. Among the live U and V entries of one group of 4 consecutive cell blocks (starting at a multiple of 4), at most 8 name wire blocks of one z-block, and every such group reaches 8 for some z-block. `ovl_count`: entry k of a list is live where k < count; the others are ignored.
All inputs are finite; a program needn't handle non-finite values.
Results may differ from the reference program's by a relative error of at most 0.0058.
Values may be sent and summed in bfloat16 or wider, within the bound.
A program may use at most 128 MiB of HBM per device.

```python
import math
import jax
import jax.numpy as jnp
from jax import lax

WIRES = 512
TICKS = 3072
RESP_W = 21
RESP_T = 200
WB = 32
TPB = 8
HB = 2
K = 2
VB = 128
NDIFF = 6
NVB = 4
WBLK = 16
X = 384
VBLK = 64
CELLS = 8192
N_GZ = 4
N_DRIFT = 4


def draw_ovl_block(key, part):
    devices = N_GZ * N_DRIFT
    per_owner = WIRES // WB // N_GZ
    cap_limit = 8 * NVB // N_GZ
    other_count = N_GZ - 1
    key_hot, key_order, key_shift, key_cross, key_local = jax.random.split(jax.random.fold_in(key, 17), 5)
    hot_rows = jax.random.randint(key_hot, (N_DRIFT,), 0, N_GZ)
    device_ids = jnp.arange(devices, dtype=jnp.int32)
    z_block = device_ids // N_DRIFT
    hot_owner = hot_rows[device_ids % N_DRIFT][:, None]
    slot_order = jax.vmap(lambda single: jax.random.permutation(single, 2 * NVB))(jax.random.split(key_order, devices))
    slot_rank = jnp.argsort(slot_order, axis=1).astype(jnp.int32)
    owner_shift = jax.random.randint(key_shift, (devices, 1), 0, other_count)
    first_owner = jnp.where(slot_rank < cap_limit, hot_owner, (hot_owner + 1 + (slot_rank - cap_limit + owner_shift) % other_count) % N_GZ)
    later_index = 2 * NVB - cap_limit + jnp.arange(2 * NVB, dtype=jnp.int32)[None, :]
    second_owner = (hot_owner + 1 + (later_index + owner_shift) % other_count) % N_GZ
    owners = jnp.stack([first_owner, second_owner], axis=-1)
    cross_blocks = owners * per_owner + jax.random.randint(key_cross, owners.shape, 0, per_owner)
    cross_blocks = cross_blocks.reshape(devices, NVB, 2, 2)
    local_blocks = z_block[:, None, None, None] * per_owner + jax.random.randint(key_local, (devices, NVB, 1, 2), 0, per_owner)
    return jnp.concatenate([cross_blocks, local_blocks], axis=2).reshape(devices * NVB, 3, 2).astype(jnp.int32)


def place_ends(result, rng, smallest, largest):
    extent = result.shape
    place = [jax.random.randint(jax.random.fold_in(rng, axis), (), 0, extent[axis]) for axis in range(len(extent))]
    result = result.at[tuple(place)].set(smallest)
    longest = extent.index(max(extent))
    place[longest] = (place[longest] + 1) % extent[longest]
    return result.at[tuple(place)].set(largest)


def level_of(key, extent, cuts, least, largest):
    loudness = 1.0
    for position, blocks in cuts:
        draws = jax.random.uniform(jax.random.fold_in(jax.random.fold_in(key, 6), position), (blocks,), jnp.float32, least / len(cuts), largest / len(cuts))
        loudness = loudness * jnp.repeat(jnp.exp(draws), extent[position] // blocks).reshape((-1,) + (1,) * (len(extent) - 1 - position))
    return loudness


def gaussian(own_key, extent, scale, reach, cuts=(), kind=jnp.bfloat16):
    array = jax.random.normal(own_key, extent, jnp.float32) * scale
    if len(cuts) > 0:
        array = level_of(own_key, extent, cuts, -0.22, 0.18) * array
    return jnp.clip(array, min=-reach, max=reach).astype(kind)


def setup_inputs(seed: int = 0, part: int = 0) -> dict:
    arg_keys = jax.random.split(jax.random.key(seed), 8)
    own_keys = jax.random.split(jax.random.fold_in(arg_keys[7], part), 8)
    return {
        "charge": jnp.clip(jnp.exp(math.log(2.0) - 3.6927934 * jax.random.uniform(own_keys[0], (CELLS, X), jnp.float32) ** level_of(own_keys[0], (CELLS, X), ((0, 16),), -0.2, 0.2)), 0.049804688, 2.0).astype(jnp.bfloat16),
        "intersection": jnp.clip(0.03125 * jax.random.uniform(own_keys[1], (VBLK, 3, K, WB, VB), jnp.float32) ** level_of(own_keys[1], (VBLK, 3, K, WB, VB), ((0, 16),), -0.2, 0.2), 0.0, 0.03125).astype(jnp.bfloat16),
        "ovl_block": draw_ovl_block(jax.random.fold_in(jax.random.fold_in(arg_keys[7], part), 71), part),
        "ovl_count": place_ends(jax.random.randint(own_keys[3], (VBLK, 3), 1, K + 1), jax.random.fold_in(own_keys[3], 1), 1, K).astype(jnp.int32),
        "diff_class": place_ends(jax.random.randint(own_keys[4], (X,), 0, NDIFF), jax.random.fold_in(own_keys[4], 1), 0, NDIFF - 1).astype(jnp.int32),
        "response": gaussian(arg_keys[5], (3, RESP_W, RESP_T), 0.005, 0.029907227),
        "cotangent": gaussian(own_keys[6], (3, WIRES, TICKS), 20.0, 120.0, ((1, 4), (2, 4))),
    }


def smear_weights(offset, classes):
    spread_width = TPB * (0.2 + 0.15 * classes)
    reach_ticks = HB * TPB
    samples = jnp.arange(-reach_ticks, reach_ticks).astype(jnp.float32) + 0.5
    normalizer = jnp.sum(jnp.exp(-(samples * samples) / (2.0 * spread_width[..., None] * spread_width[..., None])), axis=-1)
    inside = jnp.abs(offset) < reach_ticks
    bump = jnp.exp(-(offset * offset) / (2.0 * spread_width * spread_width))
    return jnp.where(inside, bump, jnp.zeros_like(bump)) / normalizer


def planes_conv(field, kernel, padding):
    return lax.conv_general_dilated(field[None], kernel[:, None], (1, 1), padding, dimension_numbers=("NCHW", "OIHW", "NCHW"), feature_group_count=3, precision=lax.Precision.HIGHEST)[0]


def reference(charge, intersection, ovl_block, ovl_count, diff_class, response, cotangent):
    highest = lax.Precision.HIGHEST
    entry_live = jnp.arange(K, dtype=jnp.int32)[None, None, :] < ovl_count[:, :, None]
    weights = intersection.astype(jnp.float32)
    charge_blocks = charge.reshape(VBLK, VB, X).astype(jnp.float32)
    pieces = jnp.einsum("bpkwc,bcx->bpkwx", weights, charge_blocks, precision=highest).astype(jnp.bfloat16)
    pieces = jnp.where(entry_live[:, :, :, None, None], pieces, jnp.zeros((), jnp.bfloat16))
    plane_of = jnp.broadcast_to(jnp.arange(3, dtype=jnp.int32)[None, :, None], ovl_block.shape)
    target = (plane_of * WBLK + ovl_block).reshape(-1).astype(jnp.int32)
    currents = jax.ops.segment_sum(pieces.reshape(VBLK * 3 * K, WB, X).astype(jnp.float32), target, num_segments=3 * WBLK)
    currents = currents.reshape(3, WIRES, X)
    bin_index = jnp.arange(X).astype(jnp.float32)
    tick_index = jnp.arange(TICKS).astype(jnp.float32)
    offset = tick_index[None, :] - TPB * bin_index[:, None] - (TPB - 1) / 2.0
    smear_table = smear_weights(offset, diff_class.astype(jnp.float32)[:, None])
    drifted = jnp.einsum("pwx,xt->pwt", currents, smear_table, precision=highest).astype(jnp.bfloat16)
    half_width = (RESP_W - 1) // 2
    response_wide = response.astype(jnp.float32)
    signal = planes_conv(drifted.astype(jnp.float32), response_wide[:, :, ::-1], [(half_width, half_width), (RESP_T - 1, 0)]).astype(jnp.bfloat16)
    tick_grads = planes_conv(cotangent.astype(jnp.float32), response_wide[:, ::-1, :], [(half_width, half_width), (0, RESP_T - 1)]).astype(jnp.bfloat16)
    bin_grads = jnp.einsum("pwt,xt->pwx", tick_grads.astype(jnp.float32), smear_table, precision=highest).astype(jnp.bfloat16)
    blocks = bin_grads.reshape(3 * WBLK, WB, X)
    chosen = jnp.take(blocks, target, axis=0).reshape(VBLK, 3, K, WB, X)
    chosen = jnp.where(entry_live[:, :, :, None, None], chosen, jnp.zeros((), jnp.bfloat16))
    charge_grad = jnp.einsum("bpkwc,bpkwx->bcx", weights, chosen.astype(jnp.float32), precision=highest)
    return signal, charge_grad.reshape(CELLS, X).astype(jnp.bfloat16)
```

```python
import functools
import math

import jax
import jax.numpy as jnp
from jax import lax
from jax.experimental import pallas as pl
from jax.experimental.pallas import tpu as pltpu
from jax.sharding import PartitionSpec as P


TPB = 8
HB = 2
LANES = 128
ROWS = 16

VMEM = pl.BlockSpec(memory_space=pltpu.VMEM)
SMEM = pl.BlockSpec(memory_space=pltpu.SMEM)


def round_up(value, step):
    return -(-value // step) * step


def iota(shape, dim):
    return lax.broadcasted_iota(jnp.int32, shape, dim)


def smear_weights(offset, classes):
    width = TPB * (0.2 + 0.15 * classes)
    reach = HB * TPB
    scale = 1.0 / (2.0 * width * width)
    normalizer = jnp.zeros_like(width)
    for j in range(-reach, reach):
        normalizer += jnp.exp(-((j + 0.5) ** 2) * scale)
    bump = jnp.exp(-(offset * offset) * scale)
    return jnp.where(jnp.abs(offset) < reach, bump, 0.0) / normalizer


def split_dot(left, right, dims):
    return lax.dot_general(
        left.astype(jnp.float32),
        right,
        (dims, ((), ())),
        precision=lax.Precision.HIGHEST,
        preferred_element_type=jnp.float32,
    )


def pieces_kernel(dims, blk_ref, count_ref, charge_ref, inter_ref, pay_ref, own_ref, seen_ref):
    owners, slabs, per_owner, capacity, bins_here, front, width, used = dims
    blocks, rows, cells = inter_ref.shape
    entries, wires = 2, rows // 6
    bins = charge_ref.shape[1]
    z_index = lax.axis_index("gz")
    x = iota((bins, slabs * width), 0)
    lane = iota((bins, slabs * width), 1)
    place = jnp.where(
        (x == (lane // width) * bins_here - front + lane % width) & (lane % width < used), 1.0, 0.0
    ).astype(jnp.bfloat16)
    pay_ref[...] = jnp.zeros_like(pay_ref)
    own_ref[...] = jnp.zeros_like(own_ref)
    for g in range(owners):
        seen_ref[g] = 0
    is_label = iota((wires, width), 1) == width - 1
    for b in range(blocks):
        framed = jnp.dot(
            charge_ref[b * cells : (b + 1) * cells], place, preferred_element_type=jnp.float32
        ).astype(jnp.bfloat16)
        piece = jnp.dot(inter_ref[b], framed, preferred_element_type=jnp.float32)
        piece = piece.astype(jnp.bfloat16).astype(jnp.float32)
        for p in range(3):
            for k in range(entries):
                e = (b * 3 + p) * entries + k
                block = blk_ref[e]
                row = (p * entries + k) * wires
                mine = piece[row : row + wires]

                @pl.when(k < count_ref[b * 3 + p])
                def _():
                    if p == 2:
                        at = pl.multiple_of((block - z_index * per_owner) * wires, wires)
                        for d in range(slabs):
                            own_ref[d, pl.ds(at, wires), :] += mine[:, d * width : (d + 1) * width]
                    else:
                        owner = block // per_owner
                        slot = seen_ref[owner]
                        seen_ref[owner] = slot + 1
                        label = (p * per_owner + block - owner * per_owner + 1).astype(jnp.float32)
                        for d in range(slabs):
                            part = jnp.where(is_label, label, mine[:, d * width : (d + 1) * width])
                            pay_ref[(owner * slabs + d) * capacity + slot] = part.astype(
                                jnp.bfloat16
                            )


def drift_kernel(dims, recv_ref, own_ref, class_ref, out_ref):
    per_owner, wires, width, _, front, lead, ticks_here = dims
    total = out_ref.shape[2]
    slab = lax.axis_index("drift")
    unroll = math.gcd(recv_ref.shape[0], 4)

    def add(step, sums):
        for u in range(unroll):
            part = recv_ref[step * unroll + u].astype(jnp.float32)
            label = part[:, width - 1 : width]
            sums = tuple(s + jnp.where(label == q + 1, part, 0.0) for q, s in enumerate(sums))
        return sums

    zero = jnp.zeros((wires, width), jnp.float32)
    sums = lax.fori_loop(0, recv_ref.shape[0] // unroll, add, (zero,) * (2 * per_owner))
    own = own_ref[0]
    for d in range(1, own_ref.shape[0]):
        own = own + own_ref[d]
    tick = iota((width, total), 1) - lead
    offset = (tick - TPB * (iota((width, total), 0) - front)).astype(jnp.float32) - (TPB - 1) / 2
    weights = smear_weights(offset, class_ref[...])
    weights = jnp.where(tick + slab * ticks_here >= 0, weights, 0.0)
    currents = jnp.concatenate(list(sums) + [own], 0)
    currents = jnp.where(iota(currents.shape, 1) == width - 1, 0.0, currents)
    drifted = split_dot(currents, weights, ((1,), (0,))).astype(jnp.bfloat16)
    here = per_owner * wires
    for p in range(3):
        out_ref[p] = drifted[p * here : (p + 1) * here]


def convolve(main_ref, prev_ref, next_ref, taps_ref, ext_ref, acc_ref, block, depth, first):
    here = main_ref.shape[1]
    count = acc_ref.shape[0] // here
    ext_ref[:ROWS] = prev_ref[0].astype(jnp.float32)
    ext_ref[ROWS : ROWS + here] = main_ref[0].astype(jnp.float32)
    ext_ref[ROWS + here :] = next_ref[0].astype(jnp.float32)
    acc_ref[...] = jnp.zeros_like(acc_ref)

    for j in range(taps_ref.shape[1]):
        shifted = ext_ref[first + j : first + j + here, :].astype(jnp.bfloat16)
        row = jnp.broadcast_to(taps_ref[0, j : j + 1, :], (block, depth))
        table = pltpu.roll(row, 0, 1, stride=1, stride_axis=0).astype(jnp.bfloat16)
        framed = jnp.concatenate(
            [shifted[:, c * block : c * block + depth] for c in range(count)], 0
        )
        acc_ref[...] += lax.dot_general(
            framed, table, (((1,), (1,)), ((), ())), preferred_element_type=jnp.float32
        )


def signal_kernel(dims, main_ref, prev_ref, next_ref, taps_ref, out_ref, ext_ref, acc_ref):
    block, depth, first = dims
    convolve(main_ref, prev_ref, next_ref, taps_ref, ext_ref, acc_ref, block, depth, first)
    here = main_ref.shape[1]
    for c in range(acc_ref.shape[0] // here):
        out_ref[0, :, c * block : (c + 1) * block] = acc_ref[c * here : (c + 1) * here].astype(
            jnp.bfloat16
        )


def bins_kernel(
    dims, main_ref, prev_ref, next_ref, taps_ref, class_ref, out_ref, ext_ref, acc_ref
):
    block, depth, first = dims
    convolve(main_ref, prev_ref, next_ref, taps_ref, ext_ref, acc_ref, block, depth, first)
    here = main_ref.shape[1]
    total = jnp.zeros(out_ref.shape[1:], jnp.float32)
    shape = (block, out_ref.shape[2])
    for c in range(acc_ref.shape[0] // here):
        ticks = acc_ref[c * here : (c + 1) * here].astype(jnp.bfloat16)
        offset = c * block + iota(shape, 0) - TPB * (iota(shape, 1) - HB)
        weights = smear_weights(offset.astype(jnp.float32) - (TPB - 1) / 2, class_ref[...])
        total += split_dot(ticks, weights, ((1,), (0,)))
    out_ref[0] = total.astype(jnp.bfloat16)


def grads_kernel(dims, blk_ref, count_ref, every_ref, inter_ref, out_ref, pick_ref):
    slabs, per_owner, bins_here, width = dims
    blocks, rows, cells = inter_ref.shape
    entries, wires = 2, rows // 6
    bins = out_ref.shape[1]
    lane = iota((slabs * width, bins), 0)
    x = iota((slabs * width, bins), 1)
    place = jnp.where(
        (x == (lane // width) * bins_here - HB + lane % width)
        & (lane % width < bins_here + 2 * HB),
        1.0,
        0.0,
    ).astype(jnp.bfloat16)
    for b in range(blocks):
        for p in range(3):
            for k in range(entries):
                block = blk_ref[(b * 3 + p) * entries + k]
                live = k < count_ref[b * 3 + p]
                owner = block // per_owner
                row = (p * entries + k) * wires
                for d in range(slabs):
                    at = ((owner * slabs + d) * 3 + p) * per_owner + block - owner * per_owner
                    part = every_ref[at]
                    pick_ref[row : row + wires, d * width : (d + 1) * width] = jnp.where(
                        live, part, jnp.zeros_like(part)
                    )
        chosen = jnp.dot(pick_ref[...], place, preferred_element_type=jnp.float32)
        out_ref[b * cells : (b + 1) * cells] = lax.dot_general(
            inter_ref[b],
            chosen.astype(jnp.bfloat16),
            (((0,), (0,)), ((), ())),
            preferred_element_type=jnp.float32,
        ).astype(jnp.bfloat16)


def moved(block, axis, distance):
    devices = range(lax.axis_size(axis))
    return lax.ppermute(
        block, axis, [(i - distance, i) for i in devices if i - distance in devices]
    )


def local(charge, intersection, ovl_block, ovl_count, diff_class, response, cotangent):
    blocks, planes, entries, wires, cells = intersection.shape
    bins = charge.shape[1]
    owners, slabs = lax.axis_size("gz"), lax.axis_size("drift")
    slab = lax.axis_index("drift")
    here, ticks_here = cotangent.shape[1:]
    per_owner = here // wires
    capacity = 8 * blocks // owners
    spread, length = response.shape[1:]
    half = (spread - 1) // 2
    first = ROWS - half
    bins_here = bins // slabs
    front = (length - 1 + HB * TPB + (TPB - 1) // 2) // TPB
    used = front + bins_here + HB
    width = round_up(used + 1, LANES)
    grad_width = round_up(bins_here + 2 * HB, LANES)
    block = math.gcd(ticks_here, 256)
    depth = round_up(block + length - 1, LANES)
    lead = depth - block
    total = ticks_here + lead
    count = ticks_here // block

    inter = intersection.reshape(blocks, planes * entries * wires, cells)
    blk = ovl_block.reshape(-1)
    cnt = ovl_count.reshape(-1)
    classes = diff_class.astype(jnp.float32)

    def class_window(lo, n):
        padded = jnp.pad(classes, (LANES * 2, LANES * 2), mode="edge")
        return lax.dynamic_slice_in_dim(padded, slab * bins_here - lo + LANES * 2, n)

    taps = response.astype(jnp.float32)
    forward_taps = jnp.pad(
        taps[:, :, ::-1], ((0, 0), (0, 0), (lead - length + 1, depth - lead - 1))
    )
    backward_taps = jnp.pad(taps[:, ::-1, :], ((0, 0), (0, 0), (0, depth - length)))

    payload, own = pl.pallas_call(
        functools.partial(
            pieces_kernel,
            (owners, slabs, per_owner, capacity, bins_here, front, width, used),
        ),
        out_shape=(
            jax.ShapeDtypeStruct((owners * slabs * capacity, wires, width), jnp.bfloat16),
            jax.ShapeDtypeStruct((slabs, here, width), jnp.float32),
        ),
        in_specs=[SMEM, SMEM, VMEM, VMEM],
        out_specs=(VMEM, VMEM),
        scratch_shapes=[pltpu.SMEM((owners,), jnp.int32)],
        name="pieces",
    )(blk, cnt, charge, inter)

    recv = lax.all_to_all(payload, ("gz", "drift"), 0, 0, tiled=True)
    own_sum = lax.psum_scatter(own, "drift", scatter_dimension=0, tiled=True)

    def plane_spec(rows, columns):
        return pl.BlockSpec((1, rows, columns), lambda p: (p, 0, 0))

    conv_specs = [
        plane_spec(here, total),
        plane_spec(ROWS, total),
        plane_spec(ROWS, total),
        plane_spec(spread, depth),
    ]
    conv_scratch = [
        pltpu.VMEM((here + 2 * ROWS, total), jnp.float32),
        pltpu.VMEM((count * here, block), jnp.float32),
    ]
    conv_cost = pl.CostEstimate(
        flops=2 * planes * spread * here * count * depth * block,
        bytes_accessed=4 * planes * here * total,
        transcendentals=0,
    )

    later = moved(cotangent[:, :, :lead], "drift", -1)
    cot = jnp.concatenate([cotangent, later], 2)
    cot_prev = moved(cot[:, here - ROWS :], "gz", 1)
    cot_next = moved(cot[:, :ROWS], "gz", -1)
    partial_bins = pl.pallas_call(
        functools.partial(bins_kernel, (block, depth, first)),
        grid=(planes,),
        out_shape=jax.ShapeDtypeStruct((planes, here, grad_width), jnp.bfloat16),
        in_specs=conv_specs + [pl.BlockSpec((1, grad_width), lambda p: (0, 0))],
        out_specs=plane_spec(here, grad_width),
        scratch_shapes=conv_scratch,
        cost_estimate=conv_cost,
        name="bins",
    )(cot, cot_prev, cot_next, backward_taps, class_window(HB, grad_width)[None, :])
    every = lax.all_gather(partial_bins, ("gz", "drift"), axis=0, tiled=True)

    drifted = pl.pallas_call(
        functools.partial(
            drift_kernel, (per_owner, wires, width, bins_here, front, lead, ticks_here)
        ),
        out_shape=jax.ShapeDtypeStruct((planes, here, total), jnp.bfloat16),
        in_specs=[VMEM, VMEM, VMEM],
        out_specs=VMEM,
        name="drift",
    )(recv, own_sum, class_window(front, width)[:, None])
    drift_prev = moved(drifted[:, here - ROWS :], "gz", 1)
    drift_next = moved(drifted[:, :ROWS], "gz", -1)
    signal = pl.pallas_call(
        functools.partial(signal_kernel, (block, depth, first)),
        grid=(planes,),
        out_shape=jax.ShapeDtypeStruct((planes, here, ticks_here), jnp.bfloat16),
        in_specs=conv_specs,
        out_specs=plane_spec(here, ticks_here),
        scratch_shapes=conv_scratch,
        cost_estimate=conv_cost,
        name="signal",
    )(drifted, drift_prev, drift_next, forward_taps)

    charge_grad = pl.pallas_call(
        functools.partial(grads_kernel, (slabs, per_owner, bins_here, grad_width)),
        out_shape=jax.ShapeDtypeStruct((blocks * cells, bins), jnp.bfloat16),
        in_specs=[SMEM, SMEM, VMEM, VMEM],
        out_specs=VMEM,
        scratch_shapes=[pltpu.VMEM((planes * entries * wires, slabs * grad_width), jnp.bfloat16)],
        name="grads",
    )(blk, cnt, every.reshape(owners * slabs * planes * per_owner, wires, grad_width), inter)
    return signal, charge_grad


def solution(mesh):
    return jax.shard_map(
        local,
        mesh=mesh,
        in_specs=(
            P(("apa", "gz", "drift"), None),
            P(("apa", "gz", "drift"), None, None, None, None),
            P(("apa", "gz", "drift"), None, None),
            P(("apa", "gz", "drift"), None),
            P("apa"),
            P(),
            P("apa", "gz", "drift"),
        ),
        out_specs=(P("apa", "gz", "drift"), P(("apa", "gz", "drift"), None)),
        check_vma=False,
    )
```
